256 devices in a mesh: gx: 16 (over z_hi, y), gy: 4 (over x), sa: 4 (over z_lo, core).
Axes of the slice: x: 4, y: 4, z: 8 (z_hi: 4, z_lo: 2; z = z_hi * 2 + z_lo), core: 2. Of those that a mesh axis runs over, the one named last changes fastest.
Arguments:
- volume: bfloat16 [4, 128, 64, 256], P('sa', 'gx', 'gy'), may hold values from -6 to 6
- first_kernel: bfloat16 [27, 128], replicated, may hold values from -0.625 to 0.625
- second_kernel: bfloat16 [27, 2048], replicated, may hold values from -0.21875 to 0.21875
- cotangent: bfloat16 [4, 32, 16, 1024], P('sa', 'gx', 'gy'), may hold values from -0.14941406 to 0.14941406
Outputs:
- stem_output: bfloat16 [4, 32, 16, 1024], P('sa', 'gx', 'gy')
- first_weights: float32 [27, 128], replicated
- second_weights: float32 [27, 2048], replicated
The draws below stay inside these ranges and needn't reach their ends.
All inputs are finite; a program needn't handle non-finite values.
Results may differ from the reference program's by a relative error of at most 0.0051.
Values may be sent and summed in bfloat16 or wider, within the bound.
A program may use at most 64 MiB of HBM per device.

```python
import jax
import jax.numpy as jnp
from jax import lax

CH_IN = 4
CH_ONE = 32
CH_TWO = 64
CZ = 64
NX = 128
NY = 64
SAMPLES = 4


def block_scale(stream_key, shape, split, low, top_value):
    def one(dim, parts):
        heights = jax.random.uniform(jax.random.fold_in(jax.random.fold_in(stream_key, 6), dim), (parts,), jnp.float32, low / len(split), top_value / len(split))
        return jnp.repeat(jnp.exp(heights), shape[dim] // parts).reshape((-1,) + (1,) * (len(shape) - dim - 1))

    loudness = one(*split[0])
    for cut in split[1:]:
        loudness = loudness * one(*cut)
    return loudness


def noise(rng, extent, scale, most, pieces=(), kind=jnp.bfloat16):
    entries = jax.random.normal(rng, extent, jnp.float32) * scale
    if len(pieces) > 0:
        entries = block_scale(rng, extent, pieces, -0.22, 0.18) * entries
    return jnp.clip(entries, min=-most, max=most).astype(kind)


def setup_inputs(seed: int = 0) -> dict:
    key_list = jax.random.split(jax.random.key(seed), 5)
    return {
        "volume": noise(key_list[0], (SAMPLES, NX, NY, CZ * CH_IN), 1.0, 6.0, ((0, 4), (1, 16), (2, 4))),
        "first_kernel": noise(key_list[1], (27, CH_IN * CH_ONE), (27 * CH_IN) ** -0.5, 0.625),
        "second_kernel": noise(key_list[2], (27, CH_ONE * CH_TWO), (27 * CH_ONE) ** -0.5, 0.21875),
        "cotangent": noise(key_list[3], (SAMPLES, NX // 4, NY // 4, (CZ // 4) * CH_TWO), 0.025, 0.14941406, ((0, 4), (1, 16), (2, 4))),
    }


def wrap_pad(values, width):
    return jnp.pad(values, ((0, 0), (width, width), (width, width), (0, 0), (0, 0)), mode="wrap")


def convolve(padded, weight):
    return lax.conv_general_dilated(padded.astype(jnp.float32), weight.astype(jnp.float32), (1, 1, 1),
                                    [(0, 0), (0, 0), (1, 1)], dimension_numbers=("NDHWC", "DHWIO", "NDHWC"),
                                    precision=lax.Precision.HIGHEST)


def weight_gradient(padded, grad):
    deeper = jnp.pad(padded.astype(jnp.float32), ((0, 0), (0, 0), (0, 0), (1, 1), (0, 0)))
    return lax.conv_general_dilated(deeper, grad.astype(jnp.float32), (1, 1, 1), "VALID",
                                    dimension_numbers=("CDHWN", "IDHWO", "DHWNC"),
                                    precision=lax.Precision.HIGHEST)


def transpose_kernel(weight):
    return jnp.transpose(weight[::-1, ::-1, ::-1], (0, 1, 2, 4, 3))


def average_pool(values):
    shape = values.shape
    blocks = values.reshape(shape[0], shape[1] // 2, 2, shape[2] // 2, 2, shape[3] // 2, 2, shape[4])
    return jnp.mean(blocks, axis=(2, 4, 6))


def upsample(values):
    return jnp.repeat(jnp.repeat(jnp.repeat(values, 2, axis=1), 2, axis=2), 2, axis=3)


def silu_slope(values):
    sigma = jax.nn.sigmoid(values)
    return sigma * (1.0 + values * (1.0 - sigma))


def reference(volume, first_kernel, second_kernel, cotangent):
    kernel_one = first_kernel.reshape(3, 3, 3, CH_IN, CH_ONE)
    kernel_two = second_kernel.reshape(3, 3, 3, CH_ONE, CH_TWO)

    def one_sample(sample):
        single = sample[0].reshape(1, NX, NY, CZ, CH_IN)
        outer_grad = sample[1].reshape(1, NX // 4, NY // 4, CZ // 4, CH_TWO)
        padded_volume = wrap_pad(single, 1)
        first_pre = convolve(padded_volume, kernel_one)
        first_pooled = average_pool(jax.nn.silu(first_pre)).astype(jnp.bfloat16)
        padded_pooled = wrap_pad(first_pooled, 1)
        second_pre = convolve(padded_pooled, kernel_two)
        result = average_pool(jax.nn.silu(second_pre)).astype(jnp.bfloat16)
        second_grad = (upsample(outer_grad.astype(jnp.float32)) * (0.125 * silu_slope(second_pre))).astype(jnp.bfloat16)
        second_weights = weight_gradient(padded_pooled, second_grad)
        pooled_grad = convolve(wrap_pad(second_grad, 1), transpose_kernel(kernel_two))
        first_grad = (upsample(pooled_grad) * (0.125 * silu_slope(first_pre))).astype(jnp.bfloat16)
        first_weights = weight_gradient(padded_volume, first_grad)
        flat = result.reshape(NX // 4, NY // 4, (CZ // 4) * CH_TWO)
        return flat, first_weights, second_weights

    outputs, first_all, second_all = lax.map(one_sample, (volume, cotangent))
    first_total = jnp.sum(first_all, axis=0).reshape(27, CH_IN * CH_ONE)
    second_total = jnp.sum(second_all, axis=0).reshape(27, CH_ONE * CH_TWO)
    return outputs, first_total, second_total
```

```python
import jax
import jax.numpy as jnp
from jax import lax
from jax.experimental import pallas as pl
from jax.experimental.pallas import tpu as pltpu
from jax.sharding import PartitionSpec as P

CH_IN = 4
CH_ONE = 32
CH_TWO = 64


def padded_2(x, sides, width):
    for axis, dim in sides:
        peers, length = (lax.axis_size(axis), x.shape[dim])
        up = [(i, (i + 1) % peers) for i in range(peers)]
        down = [(j, i) for i, j in up]
        last = lax.slice_in_dim(x, length - width, length, axis=dim)
        first = lax.slice_in_dim(x, 0, width, axis=dim)
        before = lax.ppermute(last, axis, up)
        after = lax.ppermute(first, axis, down)
        x = jnp.concatenate([before, x, after], axis=dim)
    return x


def convolve(padded, weight):
    return lax.conv_general_dilated(
        padded,
        weight,
        (1, 1, 1),
        [(0, 0), (0, 0), (1, 1)],
        dimension_numbers=("NDHWC", "DHWIO", "NDHWC"),
        preferred_element_type=jnp.float32,
    )


def weight_gradient(padded, grad):
    deeper = jnp.pad(padded, ((0, 0), (0, 0), (0, 0), (1, 1), (0, 0)))
    return lax.conv_general_dilated(
        deeper,
        grad,
        (1, 1, 1),
        "VALID",
        dimension_numbers=("CDHWN", "IDHWO", "DHWNC"),
        preferred_element_type=jnp.float32,
    )


def transpose_kernel(weight):
    return jnp.transpose(weight[::-1, ::-1, ::-1], (0, 1, 2, 4, 3))


def average_pool(values):
    shape = values.shape
    blocks = values.reshape(
        shape[0], shape[1] // 2, 2, shape[2] // 2, 2, shape[3] // 2, 2, shape[4]
    )
    return jnp.mean(blocks, axis=(2, 4, 6))


def upsample(values):
    return jnp.repeat(jnp.repeat(jnp.repeat(values, 2, axis=1), 2, axis=2), 2, axis=3)


def silu_slope(values):
    sigma = jax.nn.sigmoid(values)
    return sigma * (1.0 + values * (1.0 - sigma))

MESH = pl.DeviceIdType.MESH
CHUNK = 32


def sum_kernel(x_ref, out_ref, near, part, far, gathered, sends, recvs):
    row = lax.axis_index("gx")
    column = lax.axis_index("gy")
    sample = lax.axis_index("sa")
    me = column * 4 + sample
    barrier = pltpu.get_barrier_semaphore()

    def plane_peer(k):
        other = (me + k) % 16
        return other, (row, other // 4, other % 4)

    def row_peer(k):
        other = (row + k) % 16
        return other, (other, column, sample)

    for k in range(1, 16):
        pl.semaphore_signal(barrier, inc=1, device_id=plane_peer(k)[1], device_id_type=MESH)
        pl.semaphore_signal(barrier, inc=1, device_id=row_peer(k)[1], device_id_type=MESH)
    pl.semaphore_wait(barrier, 30)

    def send(stage, k, source, target, device):
        copy = pltpu.make_async_remote_copy(
            src_ref=source,
            dst_ref=target,
            send_sem=sends.at[stage, k],
            recv_sem=recvs.at[stage, k],
            device_id=device,
            device_id_type=MESH,
        )
        copy.start()
        return copy

    copies = []
    for k in range(1, 16):
        other, device = plane_peer(k)
        copies.append(send(0, k, x_ref.at[other], near.at[k], device))
    total = x_ref[me]
    for k in range(1, 16):
        copies[k - 1].wait_recv()
        total = total + near[k]
    part[...] = total
    far[row] = total
    second = []
    for k in range(1, 16):
        other, device = row_peer(k)
        second.append(send(1, k, part, far.at[row], device))
    for copy in second:
        copy.wait_recv()
    total = far[0]
    for k in range(1, 16):
        total = total + far[k]
    gathered[me] = total
    third = []
    for k in range(1, 16):
        other, device = plane_peer(k)
        third.append(send(2, k, gathered.at[me], gathered.at[me], device))
    for copy in third:
        copy.wait_recv()
    out_ref[...] = gathered[...]
    for copy in copies + second + third:
        copy.wait_send()


def sum_over_devices(first, second):
    filler = jnp.zeros((16 * CHUNK * 128 - first.size - second.size,), jnp.float32)
    flat = jnp.concatenate([second.reshape(-1), first.reshape(-1), filler])
    block = (16, CHUNK, 128)
    total = pl.pallas_call(
        sum_kernel,
        out_shape=jax.ShapeDtypeStruct(block, jnp.float32),
        in_specs=[pl.BlockSpec(memory_space=pltpu.VMEM)],
        out_specs=pl.BlockSpec(memory_space=pltpu.VMEM),
        scratch_shapes=[
            pltpu.VMEM(block, jnp.float32),
            pltpu.VMEM(block[1:], jnp.float32),
            pltpu.VMEM(block, jnp.float32),
            pltpu.VMEM(block, jnp.float32),
            pltpu.SemaphoreType.DMA((3, 16)),
            pltpu.SemaphoreType.DMA((3, 16)),
        ],
        compiler_params=pltpu.CompilerParams(collective_id=0, has_side_effects=True),
        name="sum_over_devices",
    )(flat.reshape(block)).reshape(-1)
    return (
        total[second.size : second.size + first.size].reshape(first.shape),
        total[: second.size].reshape(second.shape),
    )


def body(volume, first_kernel, second_kernel, cotangent):
    samples, rows_x, rows_y, merged = volume.shape
    planes = merged // CH_IN
    kernel_one = first_kernel.reshape(3, 3, 3, CH_IN, CH_ONE)
    kernel_two = second_kernel.reshape(3, 3, 3, CH_ONE, CH_TWO)
    fields = volume.reshape(samples, rows_x, rows_y, planes, CH_IN)
    outer = cotangent.reshape(samples, rows_x // 4, rows_y // 4, planes // 4, CH_TWO)
    padded_volume = padded_2(fields, (("gx", 1), ("gy", 2)), 1)
    first_pre = convolve(padded_volume, kernel_one)
    first_pooled = average_pool(jax.nn.silu(first_pre)).astype(jnp.bfloat16)
    padded_pooled = padded_2(first_pooled, (("gx", 1), ("gy", 2)), 1)
    second_pre = convolve(padded_pooled, kernel_two)
    result = average_pool(jax.nn.silu(second_pre)).astype(jnp.bfloat16)
    second_grad = (upsample(outer.astype(jnp.float32)) * (0.125 * silu_slope(second_pre))).astype(
        jnp.bfloat16
    )
    second_padded = padded_2(second_grad, (("gx", 1), ("gy", 2)), 1)
    second_weights = weight_gradient(padded_pooled, second_grad).reshape(27, CH_ONE * CH_TWO)
    pooled_grad = convolve(second_padded, transpose_kernel(kernel_two))
    first_grad = (upsample(pooled_grad) * (0.125 * silu_slope(first_pre))).astype(jnp.bfloat16)
    first_weights = weight_gradient(padded_volume, first_grad).reshape(27, CH_IN * CH_ONE)
    first_weights, second_weights = sum_over_devices(first_weights, second_weights)
    flat = result.reshape(samples, rows_x // 4, rows_y // 4, planes // 4 * CH_TWO)
    return (flat, first_weights, second_weights)


def solution(mesh):
    in_specs = (P("sa", "gx", "gy", None), P(), P(), P("sa", "gx", "gy", None))
    out_specs = (P("sa", "gx", "gy", None), P(), P())
    return jax.shard_map(body, mesh=mesh, in_specs=in_specs, out_specs=out_specs, check_vma=False)
```

```python
import jax
import jax.numpy as jnp
import numpy as np
from jax import lax
from jax.experimental import pallas as pl
from jax.experimental.pallas import tpu as pltpu
from jax.sharding import PartitionSpec as P

CH_IN = 4
CH_ONE = 32
CH_TWO = 64

MESH = pl.DeviceIdType.MESH
CHUNK = 32


def sum_kernel(x_ref, out_ref, near, part, far, gathered, sends, recvs):
    row = lax.axis_index("gx")
    column = lax.axis_index("gy")
    sample = lax.axis_index("sa")
    me = column * 4 + sample
    barrier = pltpu.get_barrier_semaphore()

    def plane_peer(k):
        other = (me + k) % 16
        return other, (row, other // 4, other % 4)

    def row_peer(k):
        other = (row + k) % 16
        return other, (other, column, sample)

    for k in range(1, 16):
        pl.semaphore_signal(barrier, inc=1, device_id=plane_peer(k)[1], device_id_type=MESH)
        pl.semaphore_signal(barrier, inc=1, device_id=row_peer(k)[1], device_id_type=MESH)
    pl.semaphore_wait(barrier, 30)

    def send(stage, k, source, target, device):
        copy = pltpu.make_async_remote_copy(
            src_ref=source,
            dst_ref=target,
            send_sem=sends.at[stage, k],
            recv_sem=recvs.at[stage, k],
            device_id=device,
            device_id_type=MESH,
        )
        copy.start()
        return copy

    copies = []
    for k in range(1, 16):
        other, device = plane_peer(k)
        copies.append(send(0, k, x_ref.at[other], near.at[k], device))
    total = x_ref[me]
    for k in range(1, 16):
        copies[k - 1].wait_recv()
        total = total + near[k]
    part[...] = total
    far[row] = total
    second = []
    for k in range(1, 16):
        other, device = row_peer(k)
        second.append(send(1, k, part, far.at[row], device))
    for copy in second:
        copy.wait_recv()
    total = far[0]
    for k in range(1, 16):
        total = total + far[k]
    gathered[me] = total
    third = []
    for k in range(1, 16):
        other, device = plane_peer(k)
        third.append(send(2, k, gathered.at[me], gathered.at[me], device))
    for copy in third:
        copy.wait_recv()
    out_ref[...] = gathered[...]
    for copy in copies + second + third:
        copy.wait_send()


def sum_over_devices(first, second):
    filler = jnp.zeros((16 * CHUNK * 128 - first.size - second.size,), jnp.float32)
    flat = jnp.concatenate([second.reshape(-1), first.reshape(-1), filler])
    block = (16, CHUNK, 128)
    total = pl.pallas_call(
        sum_kernel,
        out_shape=jax.ShapeDtypeStruct(block, jnp.float32),
        in_specs=[pl.BlockSpec(memory_space=pltpu.VMEM)],
        out_specs=pl.BlockSpec(memory_space=pltpu.VMEM),
        scratch_shapes=[
            pltpu.VMEM(block, jnp.float32),
            pltpu.VMEM(block[1:], jnp.float32),
            pltpu.VMEM(block, jnp.float32),
            pltpu.VMEM(block, jnp.float32),
            pltpu.SemaphoreType.DMA((3, 16)),
            pltpu.SemaphoreType.DMA((3, 16)),
        ],
        compiler_params=pltpu.CompilerParams(collective_id=0, has_side_effects=True),
        name="sum_over_devices",
    )(flat.reshape(block)).reshape(-1)
    return (
        total[second.size : second.size + first.size].reshape(first.shape),
        total[: second.size].reshape(second.shape),
    )


def padded_2(x, sides, width):
    for axis, dim in sides:
        peers, length = (lax.axis_size(axis), x.shape[dim])
        up = [(i, (i + 1) % peers) for i in range(peers)]
        down = [(j, i) for i, j in up]
        last = lax.slice_in_dim(x, length - width, length, axis=dim)
        first = lax.slice_in_dim(x, 0, width, axis=dim)
        before = lax.ppermute(last, axis, up)
        after = lax.ppermute(first, axis, down)
        x = jnp.concatenate([before, x, after], axis=dim)
    return x


PLANES_ONE = 16
PLANES_TWO = 4


def band(planes, inputs, outputs):
    rows = np.arange((planes + 2) * inputs)
    half = planes // 2 * outputs
    columns = np.arange(2 * half)
    plane = 2 * (columns % half // outputs) + columns // half
    masks = [rows[:, None] // inputs - plane[None, :] == c for c in range(3)]
    spread_rows = rows[:, None] % inputs == np.arange(inputs)[None, :]
    spread_columns = np.arange(outputs)[:, None] == columns[None, :] % outputs
    return np.stack(masks), spread_rows, spread_columns


def banded(kernel, planes, inputs, outputs):
    masks, spread_rows, spread_columns = band(planes, inputs, outputs)
    wide = jnp.dot(
        kernel.reshape(27 * inputs, outputs),
        jnp.asarray(spread_columns, jnp.bfloat16),
        preferred_element_type=jnp.bfloat16,
    ).reshape(9, 3, inputs, -1)
    spread_rows = jnp.asarray(spread_rows, jnp.bfloat16)
    full = jnp.einsum("ri,kcin->kcrn", spread_rows, wide, preferred_element_type=jnp.bfloat16)
    full = jnp.where(masks[None], full, jnp.bfloat16(0)).sum(axis=1, dtype=jnp.bfloat16)
    return full.reshape(3, 3, full.shape[1], full.shape[2])


def unbanded(grad, planes, inputs, outputs):
    masks, spread_rows, spread_columns = band(planes, inputs, outputs)
    grad = grad.reshape(9, planes + 2, inputs, -1)
    masks = masks.reshape(3, planes + 2, inputs, -1)
    parts = [jnp.where(masks[c][None], grad, 0.0).sum(axis=1) for c in range(3)]
    narrow = jnp.stack(parts, axis=1).reshape(27 * inputs, -1)
    narrow = jnp.dot(
        narrow,
        jnp.asarray(spread_columns.T, jnp.float32),
        precision=lax.Precision.HIGHEST,
        preferred_element_type=jnp.float32,
    )
    return narrow.reshape(27, inputs * outputs)


def convolve(padded, weight, padding="VALID", form="HWIO"):
    return lax.conv_general_dilated(
        padded,
        weight,
        (1, 1),
        padding,
        dimension_numbers=("NHWC", form, "NHWC"),
        preferred_element_type=jnp.float32,
    )


def weight_gradient(padded, grad):
    return lax.conv_general_dilated(
        padded,
        grad,
        (1, 1),
        "VALID",
        dimension_numbers=("CHWN", "IHWO", "HWNC"),
        preferred_element_type=jnp.float32,
    )


def average_pool(values):
    batch, rows_x, rows_y, lanes = values.shape
    values = values[..., : lanes // 2] + values[..., lanes // 2 :]
    values = values.reshape(batch, rows_x // 2, 2, rows_y // 2, 2, lanes // 2)
    return values.sum(axis=(2, 4)) * 0.125


def upsample(values):
    values = jnp.repeat(jnp.repeat(values, 2, axis=1), 2, axis=2)
    return jnp.concatenate([values, values], axis=-1)


def chunks(values, width, margin, count):
    step = width - 2 * margin
    values = jnp.pad(values, ((0, 0), (0, 0), (margin, margin)))
    return jnp.stack([values[..., j * step : j * step + width] for j in range(count)])


def merge(values):
    return jnp.concatenate(list(values), axis=-1)


def silu_slope(values):
    sigma = jax.nn.sigmoid(values)
    return sigma * (1.0 + values * (1.0 - sigma))


def body(volume, first_kernel, second_kernel, cotangent):
    sides = (("gx", 0), ("gy", 1))
    weight_one = banded(first_kernel, PLANES_ONE, CH_IN, CH_ONE)
    weight_two = banded(second_kernel, PLANES_TWO, CH_ONE, CH_TWO)
    outer = padded_2(cotangent[0], sides, 1)
    fields = padded_2(volume[0], sides, 5)
    count = fields.shape[-1] // (PLANES_ONE * CH_IN)
    fields = chunks(fields, (PLANES_ONE + 2) * CH_IN, CH_IN, count)
    first_pre = convolve(fields, weight_one)
    pooled = merge(average_pool(jax.nn.silu(first_pre)).astype(jnp.bfloat16))
    pooled = chunks(pooled, (PLANES_TWO + 2) * CH_ONE, CH_ONE, 2 * count)
    second_pre = convolve(pooled, weight_two)
    inner = second_pre[:, 1:-1, 1:-1]
    result = merge(average_pool(jax.nn.silu(inner)).astype(jnp.bfloat16))
    outer = jnp.stack(jnp.split(outer, 2 * count, axis=-1))
    outer = upsample(outer)[:, 1:-1, 1:-1].astype(jnp.float32)
    second_grad = (outer * (0.125 * silu_slope(second_pre))).astype(jnp.bfloat16)
    grad_two = weight_gradient(pooled[:, 1:-1, 1:-1], second_grad[:, 1:-1, 1:-1])
    second_weights = unbanded(grad_two, PLANES_TWO, CH_ONE, CH_TWO)
    spread = convolve(second_grad, weight_two[::-1, ::-1], form="HWOI")
    middle = merge(spread[..., CH_ONE:-CH_ONE])
    below = jnp.pad(spread[1:, ..., :CH_ONE], ((0, 1), (0, 0), (0, 0), (0, 0)))
    above = jnp.pad(spread[:-1, ..., -CH_ONE:], ((1, 0), (0, 0), (0, 0), (0, 0)))
    room = ((0, 0), (0, 0), (0, 0))
    width = (PLANES_TWO - 1) * CH_ONE
    middle = middle + merge(jnp.pad(below, room + ((width, 0),)))
    middle = middle + merge(jnp.pad(above, room + ((0, width),)))
    pooled_grad = jnp.stack(jnp.split(middle, count, axis=-1))
    slope = 0.125 * silu_slope(first_pre[:, 4:-4, 4:-4])
    first_grad = (upsample(pooled_grad) * slope).astype(jnp.bfloat16)
    grad_one = weight_gradient(fields[:, 4:-4, 4:-4], first_grad)
    first_weights = unbanded(grad_one, PLANES_ONE, CH_IN, CH_ONE)
    first_weights, second_weights = sum_over_devices(first_weights, second_weights)
    return (result[None], first_weights, second_weights)


def solution(mesh):
    in_specs = (P("sa", "gx", "gy", None), P(), P(), P("sa", "gx", "gy", None))
    out_specs = (P("sa", "gx", "gy", None), P(), P())
    return jax.shard_map(body, mesh=mesh, in_specs=in_specs, out_specs=out_specs, check_vma=False)
```

```python
import jax
import jax.numpy as jnp
import numpy as np
from jax import lax
from jax.experimental import pallas as pl
from jax.experimental.pallas import tpu as pltpu
from jax.sharding import PartitionSpec as P

CH_IN = 4
CH_ONE = 32
CH_TWO = 64

MESH = pl.DeviceIdType.MESH
CHUNK = 32


def sum_kernel(first, second, first_out, second_out, x_ref, near, part, far, gathered, sends, recvs):
    row = lax.axis_index("gx")
    column = lax.axis_index("gy")
    sample = lax.axis_index("sa")
    me = column * 4 + sample
    barrier = pltpu.get_barrier_semaphore()

    def plane_peer(k):
        other = (me + k) % 16
        return other, (row, other // 4, other % 4)

    def row_peer(k):
        other = (row + k) % 16
        return other, (other, column, sample)

    for k in range(1, 16):
        pl.semaphore_signal(barrier, inc=1, device_id=plane_peer(k)[1], device_id_type=MESH)
        pl.semaphore_signal(barrier, inc=1, device_id=row_peer(k)[1], device_id_type=MESH)
    x_ref[...] = jnp.zeros_like(x_ref)
    for g in range(16):
        x_ref[g, 0:27] = second[:, 128 * g : 128 * g + 128]
        rows = min(2, 27 - 2 * g)
        if rows > 0:
            x_ref[g, 27 : 27 + rows] = first[2 * g : 2 * g + rows]
    pl.semaphore_wait(barrier, 30)

    def send(stage, k, source, target, device):
        copy = pltpu.make_async_remote_copy(
            src_ref=source,
            dst_ref=target,
            send_sem=sends.at[stage, k],
            recv_sem=recvs.at[stage, k],
            device_id=device,
            device_id_type=MESH,
        )
        copy.start()
        return copy

    copies = []
    for k in range(1, 16):
        other, device = plane_peer(k)
        copies.append(send(0, k, x_ref.at[other], near.at[k], device))
    total = x_ref[me]
    for k in range(1, 16):
        copies[k - 1].wait_recv()
        total = total + near[k]
    part[...] = total
    far[row] = total
    second = []
    for k in range(1, 16):
        other, device = row_peer(k)
        second.append(send(1, k, part, far.at[row], device))
    for copy in second:
        copy.wait_recv()
    total = far[0]
    for k in range(1, 16):
        total = total + far[k]
    gathered[me] = total
    third = []
    for k in range(1, 16):
        other, device = plane_peer(k)
        third.append(send(2, k, gathered.at[me], gathered.at[me], device))
    for copy in third:
        copy.wait_recv()
    for g in range(16):
        second_out[:, 128 * g : 128 * g + 128] = gathered[g, 0:27]
        rows = min(2, 27 - 2 * g)
        if rows > 0:
            first_out[2 * g : 2 * g + rows] = gathered[g, 27 : 27 + rows]
    for copy in copies + second + third:
        copy.wait_send()


def sum_over_devices(first, second):
    block = (16, CHUNK, 128)
    whole = pl.BlockSpec(memory_space=pltpu.VMEM)
    return pl.pallas_call(
        sum_kernel,
        out_shape=(
            jax.ShapeDtypeStruct(first.shape, jnp.float32),
            jax.ShapeDtypeStruct(second.shape, jnp.float32),
        ),
        in_specs=[whole, whole],
        out_specs=(whole, whole),
        scratch_shapes=[
            pltpu.VMEM(block, jnp.float32),
            pltpu.VMEM(block, jnp.float32),
            pltpu.VMEM(block[1:], jnp.float32),
            pltpu.VMEM(block, jnp.float32),
            pltpu.VMEM(block, jnp.float32),
            pltpu.SemaphoreType.DMA((3, 16)),
            pltpu.SemaphoreType.DMA((3, 16)),
        ],
        compiler_params=pltpu.CompilerParams(collective_id=0, has_side_effects=True),
        name="sum_over_devices",
    )(first, second)


def halo_kernel(volume, low, high, outer, outer_low, outer_high, *refs):
    outs, slots, sends, recvs = refs[:8], refs[8:16], refs[16], refs[17]
    row = lax.axis_index("gx")
    column = lax.axis_index("gy")
    sample = lax.axis_index("sa")
    rows = lax.axis_size("gx")
    columns = lax.axis_size("gy")

    def device(dx, dy):
        return ((row + rows + dx) % rows, (column + columns + dy) % columns, sample)

    barrier = pltpu.get_barrier_semaphore()
    around = [(dx, dy) for dx in (-1, 0, 1) for dy in (-1, 0, 1) if (dx, dy) != (0, 0)]
    for dx, dy in around:
        pl.semaphore_signal(barrier, inc=1, device_id=device(dx, dy), device_id_type=MESH)
    pl.semaphore_wait(barrier, 8)
    copies = []

    def send(source, target, dx, dy):
        k = len(copies)
        copy = pltpu.make_async_remote_copy(
            src_ref=source,
            dst_ref=target,
            send_sem=sends.at[k],
            recv_sem=recvs.at[k],
            device_id=device(dx, dy),
            device_id_type=MESH,
        )
        copy.start()
        copies.append(copy)

    groups = (
        (volume, low, high, slots[:4]),
        (outer, outer_low, outer_high, slots[4:]),
    )
    for whole, first, last, (left, right, top, bottom) in groups:
        size = whole.shape[0]
        width = top.shape[0]
        tail = pl.ds(size - width, width)
        head = pl.ds(0, width)
        end = pl.ds(size + width, width)
        send(whole.at[tail], top, 1, 0)
        send(whole.at[head], bottom, -1, 0)
        send(last, left.at[pl.ds(width, size)], 0, 1)
        send(first, right.at[pl.ds(width, size)], 0, -1)
        send(last.at[tail], left.at[head], 1, 1)
        send(last.at[head], left.at[end], -1, 1)
        send(first.at[tail], right.at[head], 1, -1)
        send(first.at[head], right.at[end], -1, -1)
    for copy in copies:
        copy.wait_recv()
    for out, slot in zip(outs, slots):
        out[...] = slot[...]
    for copy in copies:
        copy.wait_send()


def exchange(volume, outer):
    args = []
    shapes = []
    for x, width in ((volume, 5), (outer, 1)):
        rows, columns, lanes = x.shape
        args += [x, x[:, :width], x[:, columns - width :]]
        shapes += [(rows + 2 * width, width, lanes)] * 2 + [(width, columns, lanes)] * 2
    space = pl.BlockSpec(memory_space=pltpu.VMEM)
    pieces = pl.pallas_call(
        halo_kernel,
        out_shape=tuple(jax.ShapeDtypeStruct(shape, jnp.bfloat16) for shape in shapes),
        in_specs=[space] * 6,
        out_specs=(space,) * 8,
        scratch_shapes=[pltpu.VMEM(shape, jnp.bfloat16) for shape in shapes]
        + [pltpu.SemaphoreType.DMA((16,)), pltpu.SemaphoreType.DMA((16,))],
        compiler_params=pltpu.CompilerParams(collective_id=1, has_side_effects=True),
        name="exchange",
    )(*args)
    result = []
    for x, (left, right, top, bottom) in ((volume, pieces[:4]), (outer, pieces[4:])):
        middle = jnp.concatenate([top, x, bottom], axis=0)
        result.append(jnp.concatenate([left, middle, right], axis=1))
    return result


PLANES_ONE = 16
PLANES_TWO = 4


def band(planes, inputs, outputs):
    rows = np.arange((planes + 2) * inputs)
    half = planes // 2 * outputs
    columns = np.arange(2 * half)
    plane = 2 * (columns % half // outputs) + columns // half
    masks = [rows[:, None] // inputs - plane[None, :] == c for c in range(3)]
    spread_rows = rows[:, None] % inputs == np.arange(inputs)[None, :]
    spread_columns = np.arange(outputs)[:, None] == columns[None, :] % outputs
    return np.stack(masks), spread_rows, spread_columns


def banded(kernel, planes, inputs, outputs):
    masks, spread_rows, spread_columns = band(planes, inputs, outputs)
    wide = jnp.dot(
        kernel.reshape(27 * inputs, outputs),
        jnp.asarray(spread_columns, jnp.bfloat16),
        preferred_element_type=jnp.bfloat16,
    ).reshape(9, 3, inputs, -1)
    spread_rows = jnp.asarray(spread_rows, jnp.bfloat16)
    full = jnp.einsum("ri,kcin->kcrn", spread_rows, wide, preferred_element_type=jnp.bfloat16)
    full = jnp.where(masks[None], full, jnp.bfloat16(0)).sum(axis=1, dtype=jnp.bfloat16)
    return full.reshape(3, 3, full.shape[1], full.shape[2])


def unbanded(grad, planes, inputs, outputs):
    masks, spread_rows, spread_columns = band(planes, inputs, outputs)
    grad = grad.reshape(9, planes + 2, inputs, -1)
    masks = masks.reshape(3, planes + 2, inputs, -1)
    parts = [jnp.where(masks[c][None], grad, 0.0).sum(axis=1) for c in range(3)]
    narrow = jnp.stack(parts, axis=1).reshape(27 * inputs, -1)
    narrow = jnp.dot(
        narrow,
        jnp.asarray(spread_columns.T, jnp.float32),
        precision=lax.Precision.HIGHEST,
        preferred_element_type=jnp.float32,
    )
    return narrow.reshape(27, inputs * outputs)


def convolve(padded, weight, padding="VALID", form="HWIO"):
    return lax.conv_general_dilated(
        padded,
        weight,
        (1, 1),
        padding,
        dimension_numbers=("NHWC", form, "NHWC"),
        preferred_element_type=jnp.float32,
    )


def weight_gradient(padded, grad):
    return lax.conv_general_dilated(
        padded,
        grad,
        (1, 1),
        "VALID",
        dimension_numbers=("CHWN", "IHWO", "HWNC"),
        preferred_element_type=jnp.float32,
    )


def average_pool(values):
    batch, rows_x, rows_y, lanes = values.shape
    values = values[..., : lanes // 2] + values[..., lanes // 2 :]
    values = values.reshape(batch, rows_x // 2, 2, rows_y // 2, 2, lanes // 2)
    return values.sum(axis=(2, 4)) * 0.125


def upsample(values):
    values = jnp.repeat(jnp.repeat(values, 2, axis=1), 2, axis=2)
    return jnp.concatenate([values, values], axis=-1)


def chunks(values, width, margin, count):
    step = width - 2 * margin
    values = jnp.pad(values, ((0, 0), (0, 0), (margin, margin)))
    return jnp.stack([values[..., j * step : j * step + width] for j in range(count)])


def merge(values):
    return jnp.concatenate(list(values), axis=-1)


def silu_slope(values):
    sigma = jax.nn.sigmoid(values)
    return sigma * (1.0 + values * (1.0 - sigma))


def body(volume, first_kernel, second_kernel, cotangent):
    weight_one = banded(first_kernel, PLANES_ONE, CH_IN, CH_ONE)
    weight_two = banded(second_kernel, PLANES_TWO, CH_ONE, CH_TWO)
    fields, outer = exchange(volume[0], cotangent[0])
    count = fields.shape[-1] // (PLANES_ONE * CH_IN)
    fields = chunks(fields, (PLANES_ONE + 2) * CH_IN, CH_IN, count)
    first_pre = convolve(fields, weight_one)
    pooled = merge(average_pool(jax.nn.silu(first_pre)).astype(jnp.bfloat16))
    pooled = chunks(pooled, (PLANES_TWO + 2) * CH_ONE, CH_ONE, 2 * count)
    second_pre = convolve(pooled, weight_two)
    inner = second_pre[:, 1:-1, 1:-1]
    result = merge(average_pool(jax.nn.silu(inner)).astype(jnp.bfloat16))
    outer = jnp.stack(jnp.split(outer, 2 * count, axis=-1))
    outer = upsample(outer)[:, 1:-1, 1:-1].astype(jnp.float32)
    second_grad = (outer * (0.125 * silu_slope(second_pre))).astype(jnp.bfloat16)
    grad_two = weight_gradient(pooled[:, 1:-1, 1:-1], second_grad[:, 1:-1, 1:-1])
    second_weights = unbanded(grad_two, PLANES_TWO, CH_ONE, CH_TWO)
    spread = convolve(second_grad, weight_two[::-1, ::-1], form="HWOI")
    middle = merge(spread[..., CH_ONE:-CH_ONE])
    below = jnp.pad(spread[1:, ..., :CH_ONE], ((0, 1), (0, 0), (0, 0), (0, 0)))
    above = jnp.pad(spread[:-1, ..., -CH_ONE:], ((1, 0), (0, 0), (0, 0), (0, 0)))
    room = ((0, 0), (0, 0), (0, 0))
    width = (PLANES_TWO - 1) * CH_ONE
    middle = middle + merge(jnp.pad(below, room + ((width, 0),)))
    middle = middle + merge(jnp.pad(above, room + ((0, width),)))
    pooled_grad = jnp.stack(jnp.split(middle, count, axis=-1))
    slope = 0.125 * silu_slope(first_pre[:, 4:-4, 4:-4])
    first_grad = (upsample(pooled_grad) * slope).astype(jnp.bfloat16)
    grad_one = weight_gradient(fields[:, 4:-4, 4:-4], first_grad)
    first_weights = unbanded(grad_one, PLANES_ONE, CH_IN, CH_ONE)
    first_weights, second_weights = sum_over_devices(first_weights, second_weights)
    return (result[None], first_weights, second_weights)


def solution(mesh):
    in_specs = (P("sa", "gx", "gy", None), P(), P(), P("sa", "gx", "gy", None))
    out_specs = (P("sa", "gx", "gy", None), P(), P())
    return jax.shard_map(body, mesh=mesh, in_specs=in_specs, out_specs=out_specs, check_vma=False)
```

```python
import jax
import jax.numpy as jnp
import numpy as np
from jax import lax
from jax.experimental import pallas as pl
from jax.experimental.pallas import tpu as pltpu
from jax.sharding import PartitionSpec as P

CH_IN = 4
CH_ONE = 32
CH_TWO = 64

MESH = pl.DeviceIdType.MESH
PART = (4, 8, 128)


def sum_kernel(
    first, second, first_out, second_out, x_ref, near, part, quad, own, deep, spread, gathered, sends, recvs
):
    row = lax.axis_index("gx")
    column = lax.axis_index("gy")
    sample = lax.axis_index("sa")
    me = column * 4 + sample
    high = row // 4
    low = row % 4
    barrier = pltpu.get_barrier_semaphore()

    def plane_peer(k):
        other = (me + k) % 16
        return other, (row, other // 4, other % 4)

    def low_peer(k):
        other = (low + k) % 4
        return other, (high * 4 + other, column, sample)

    def high_peer(k):
        other = (high + k) % 4
        return other, (other * 4 + low, column, sample)

    for peer, count in ((plane_peer, 16), (low_peer, 4), (high_peer, 4)):
        for k in range(1, count):
            pl.semaphore_signal(barrier, inc=1, device_id=peer(k)[1], device_id_type=MESH)
    x_ref[...] = jnp.zeros_like(x_ref)
    for g in range(16):
        lanes = slice(128 * g, 128 * g + 128)
        for q in range(3):
            x_ref[g, q] = second[8 * q : 8 * q + 8, lanes]
        x_ref[g, 3, 0:3] = second[24:27, lanes]
        rows = min(2, 27 - 2 * g)
        if rows > 0:
            x_ref[g, 3, 3 : 3 + rows] = first[2 * g : 2 * g + rows]
    pl.semaphore_wait(barrier, 21)

    def send(stage, k, source, target, device):
        copy = pltpu.make_async_remote_copy(
            src_ref=source,
            dst_ref=target,
            send_sem=sends.at[stage, k],
            recv_sem=recvs.at[stage, k],
            device_id=device,
            device_id_type=MESH,
        )
        copy.start()
        return copy

    copies = []
    for k in range(1, 16):
        other, device = plane_peer(k)
        copies.append(send(0, k, x_ref.at[other], near.at[k], device))
    total = x_ref[me]
    for k in range(1, 16):
        copies[k - 1].wait_recv()
        total = total + near[k]
    part[...] = total
    second_copies = []
    for k in range(1, 4):
        other, device = low_peer(k)
        second_copies.append(send(1, k, part.at[other], quad.at[k], device))
    total = part[low]
    for k in range(1, 4):
        second_copies[k - 1].wait_recv()
        total = total + quad[k]
    own[...] = total
    deep[high] = total
    third_copies = []
    for k in range(1, 4):
        other, device = high_peer(k)
        third_copies.append(send(2, k, own, deep.at[high], device))
    for copy in third_copies:
        copy.wait_recv()
    spread[low] = (deep[0] + deep[1]) + (deep[2] + deep[3])
    fourth_copies = []
    for k in range(1, 4):
        other, device = low_peer(k)
        fourth_copies.append(send(3, k, spread.at[low], spread.at[low], device))
    for copy in fourth_copies:
        copy.wait_recv()
    last_copies = []
    for k in range(1, 16):
        other, device = plane_peer(k)
        last_copies.append(send(4, k, spread, gathered.at[me], device))
    gathered[me] = spread[...]
    for copy in last_copies:
        copy.wait_recv()
    for g in range(16):
        lanes = slice(128 * g, 128 * g + 128)
        for q in range(3):
            second_out[8 * q : 8 * q + 8, lanes] = gathered[g, q]
        second_out[24:27, lanes] = gathered[g, 3, 0:3]
        rows = min(2, 27 - 2 * g)
        if rows > 0:
            first_out[2 * g : 2 * g + rows] = gathered[g, 3, 3 : 3 + rows]
    for copy in copies + second_copies + third_copies + fourth_copies + last_copies:
        copy.wait_send()


def sum_over_devices(first, second):
    block = (16,) + PART
    whole = pl.BlockSpec(memory_space=pltpu.VMEM)
    return pl.pallas_call(
        sum_kernel,
        out_shape=(
            jax.ShapeDtypeStruct(first.shape, jnp.float32),
            jax.ShapeDtypeStruct(second.shape, jnp.float32),
        ),
        in_specs=[whole, whole],
        out_specs=(whole, whole),
        scratch_shapes=[
            pltpu.VMEM(block, jnp.float32),
            pltpu.VMEM(block, jnp.float32),
            pltpu.VMEM(PART, jnp.float32),
            pltpu.VMEM(PART, jnp.float32),
            pltpu.VMEM(PART[1:], jnp.float32),
            pltpu.VMEM(PART, jnp.float32),
            pltpu.VMEM(PART, jnp.float32),
            pltpu.VMEM(block, jnp.float32),
            pltpu.SemaphoreType.DMA((5, 16)),
            pltpu.SemaphoreType.DMA((5, 16)),
        ],
        compiler_params=pltpu.CompilerParams(collective_id=0, has_side_effects=True),
        name="sum_over_devices",
    )(first, second)


def halo_kernel(volume, outer, *refs):
    outs, slots, edges, sends, recvs = refs[:8], refs[8:16], refs[16:20], refs[20], refs[21]
    row = lax.axis_index("gx")
    column = lax.axis_index("gy")
    sample = lax.axis_index("sa")
    rows = lax.axis_size("gx")
    columns = lax.axis_size("gy")

    def device(dx, dy):
        return ((row + rows + dx) % rows, (column + columns + dy) % columns, sample)

    barrier = pltpu.get_barrier_semaphore()
    around = [(dx, dy) for dx in (-1, 0, 1) for dy in (-1, 0, 1) if (dx, dy) != (0, 0)]
    for dx, dy in around:
        pl.semaphore_signal(barrier, inc=1, device_id=device(dx, dy), device_id_type=MESH)
    for whole, first, last in ((volume, *edges[:2]), (outer, *edges[2:])):
        width = first.shape[1]
        first[...] = whole[:, :width]
        last[...] = whole[:, whole.shape[1] - width :]
    pl.semaphore_wait(barrier, 8)
    copies = []

    def send(source, target, dx, dy):
        k = len(copies)
        copy = pltpu.make_async_remote_copy(
            src_ref=source,
            dst_ref=target,
            send_sem=sends.at[k],
            recv_sem=recvs.at[k],
            device_id=device(dx, dy),
            device_id_type=MESH,
        )
        copy.start()
        copies.append(copy)

    groups = (
        (volume, *edges[:2], slots[:4]),
        (outer, *edges[2:], slots[4:]),
    )
    for whole, first, last, (left, right, top, bottom) in groups:
        size = whole.shape[0]
        width = top.shape[0]
        tail = pl.ds(size - width, width)
        head = pl.ds(0, width)
        end = pl.ds(size + width, width)
        send(whole.at[tail], top, 1, 0)
        send(whole.at[head], bottom, -1, 0)
        send(last, left.at[pl.ds(width, size)], 0, 1)
        send(first, right.at[pl.ds(width, size)], 0, -1)
        send(last.at[tail], left.at[head], 1, 1)
        send(last.at[head], left.at[end], -1, 1)
        send(first.at[tail], right.at[head], 1, -1)
        send(first.at[head], right.at[end], -1, -1)
    for copy in copies:
        copy.wait_recv()
    for out, slot in zip(outs, slots):
        out[...] = slot[...]
    for copy in copies:
        copy.wait_send()


def exchange(volume, outer):
    shapes = []
    edges = []
    for x, width in ((volume, 5), (outer, 1)):
        rows, columns, lanes = x.shape
        edges += [(rows, width, lanes)] * 2
        shapes += [(rows + 2 * width, width, lanes)] * 2 + [(width, columns, lanes)] * 2
    space = pl.BlockSpec(memory_space=pltpu.VMEM)
    pieces = pl.pallas_call(
        halo_kernel,
        out_shape=tuple(jax.ShapeDtypeStruct(shape, jnp.bfloat16) for shape in shapes),
        in_specs=[space] * 2,
        out_specs=(space,) * 8,
        scratch_shapes=[pltpu.VMEM(shape, jnp.bfloat16) for shape in shapes + edges]
        + [pltpu.SemaphoreType.DMA((16,)), pltpu.SemaphoreType.DMA((16,))],
        compiler_params=pltpu.CompilerParams(collective_id=1, has_side_effects=True),
        name="exchange",
    )(volume, outer)
    result = []
    for x, (left, right, top, bottom) in ((volume, pieces[:4]), (outer, pieces[4:])):
        middle = jnp.concatenate([top, x, bottom], axis=0)
        result.append(jnp.concatenate([left, middle, right], axis=1))
    return result


PLANES_ONE = 16
PLANES_TWO = 4


def band(planes, inputs, outputs):
    rows = np.arange((planes + 2) * inputs)
    half = planes // 2 * outputs
    columns = np.arange(2 * half)
    plane = 2 * (columns % half // outputs) + columns // half
    masks = [rows[:, None] // inputs - plane[None, :] == c for c in range(3)]
    spread_rows = rows[:, None] % inputs == np.arange(inputs)[None, :]
    spread_columns = np.arange(outputs)[:, None] == columns[None, :] % outputs
    return np.stack(masks), spread_rows, spread_columns


def banded(kernel, planes, inputs, outputs):
    masks, spread_rows, spread_columns = band(planes, inputs, outputs)
    wide = jnp.dot(
        kernel.reshape(27 * inputs, outputs),
        jnp.asarray(spread_columns, jnp.bfloat16),
        preferred_element_type=jnp.bfloat16,
    ).reshape(9, 3, inputs, -1)
    spread_rows = jnp.asarray(spread_rows, jnp.bfloat16)
    full = jnp.einsum("ri,kcin->kcrn", spread_rows, wide, preferred_element_type=jnp.bfloat16)
    full = jnp.where(masks[None], full, jnp.bfloat16(0)).sum(axis=1, dtype=jnp.bfloat16)
    return full.reshape(3, 3, full.shape[1], full.shape[2])


def unbanded(grad, planes, inputs, outputs):
    masks, spread_rows, spread_columns = band(planes, inputs, outputs)
    grad = grad.reshape(9, planes + 2, inputs, -1)
    masks = masks.reshape(3, planes + 2, inputs, -1)
    parts = [jnp.where(masks[c][None], grad, 0.0).sum(axis=1) for c in range(3)]
    narrow = jnp.stack(parts, axis=1).reshape(27 * inputs, -1)
    narrow = jnp.dot(
        narrow,
        jnp.asarray(spread_columns.T, jnp.float32),
        precision=lax.Precision.HIGHEST,
        preferred_element_type=jnp.float32,
    )
    return narrow.reshape(27, inputs * outputs)


def convolve(padded, weight, padding="VALID", form="HWIO"):
    return lax.conv_general_dilated(
        padded,
        weight,
        (1, 1),
        padding,
        dimension_numbers=("NHWC", form, "NHWC"),
        preferred_element_type=jnp.float32,
    )


def weight_gradient(padded, grad):
    return lax.conv_general_dilated(
        padded,
        grad,
        (1, 1),
        "VALID",
        dimension_numbers=("CHWN", "IHWO", "HWNC"),
        preferred_element_type=jnp.float32,
    )


def average_pool(values):
    batch, rows_x, rows_y, lanes = values.shape
    values = values[..., : lanes // 2] + values[..., lanes // 2 :]
    values = values.reshape(batch, rows_x // 2, 2, rows_y // 2, 2, lanes // 2)
    return values.sum(axis=(2, 4)) * 0.125


def upsample(values):
    values = jnp.repeat(jnp.repeat(values, 2, axis=1), 2, axis=2)
    return jnp.concatenate([values, values], axis=-1)


def chunks(values, width, margin, count):
    step = width - 2 * margin
    values = jnp.pad(values, ((0, 0), (0, 0), (margin, margin)))
    return jnp.stack([values[..., j * step : j * step + width] for j in range(count)])


def merge(values):
    return jnp.concatenate(list(values), axis=-1)


def silu_slope(values):
    sigma = jax.nn.sigmoid(values)
    return sigma * (1.0 + values * (1.0 - sigma))


def body(volume, first_kernel, second_kernel, cotangent):
    weight_one = banded(first_kernel, PLANES_ONE, CH_IN, CH_ONE)
    weight_two = banded(second_kernel, PLANES_TWO, CH_ONE, CH_TWO)
    fields, outer = exchange(volume[0], cotangent[0])
    count = fields.shape[-1] // (PLANES_ONE * CH_IN)
    fields = chunks(fields, (PLANES_ONE + 2) * CH_IN, CH_IN, count)
    first_pre = convolve(fields, weight_one)
    pooled = merge(average_pool(jax.nn.silu(first_pre)).astype(jnp.bfloat16))
    pooled = chunks(pooled, (PLANES_TWO + 2) * CH_ONE, CH_ONE, 2 * count)
    second_pre = convolve(pooled, weight_two)
    inner = second_pre[:, 1:-1, 1:-1]
    result = merge(average_pool(jax.nn.silu(inner)).astype(jnp.bfloat16))
    outer = jnp.stack(jnp.split(outer, 2 * count, axis=-1))
    outer = upsample(outer)[:, 1:-1, 1:-1].astype(jnp.float32)
    second_grad = (outer * (0.125 * silu_slope(second_pre))).astype(jnp.bfloat16)
    grad_two = weight_gradient(pooled[:, 1:-1, 1:-1], second_grad[:, 1:-1, 1:-1])
    second_weights = unbanded(grad_two, PLANES_TWO, CH_ONE, CH_TWO)
    spread = convolve(second_grad, weight_two[::-1, ::-1], form="HWOI")
    middle = merge(spread[..., CH_ONE:-CH_ONE])
    below = jnp.pad(spread[1:, ..., :CH_ONE], ((0, 1), (0, 0), (0, 0), (0, 0)))
    above = jnp.pad(spread[:-1, ..., -CH_ONE:], ((1, 0), (0, 0), (0, 0), (0, 0)))
    room = ((0, 0), (0, 0), (0, 0))
    width = (PLANES_TWO - 1) * CH_ONE
    middle = middle + merge(jnp.pad(below, room + ((width, 0),)))
    middle = middle + merge(jnp.pad(above, room + ((0, width),)))
    pooled_grad = jnp.stack(jnp.split(middle, count, axis=-1))
    slope = 0.125 * silu_slope(first_pre[:, 4:-4, 4:-4])
    first_grad = (upsample(pooled_grad) * slope).astype(jnp.bfloat16)
    grad_one = weight_gradient(fields[:, 4:-4, 4:-4], first_grad)
    first_weights = unbanded(grad_one, PLANES_ONE, CH_IN, CH_ONE)
    first_weights, second_weights = sum_over_devices(first_weights, second_weights)
    return (result[None], first_weights, second_weights)


def solution(mesh):
    in_specs = (P("sa", "gx", "gy", None), P(), P(), P("sa", "gx", "gy", None))
    out_specs = (P("sa", "gx", "gy", None), P(), P())
    return jax.shard_map(body, mesh=mesh, in_specs=in_specs, out_specs=out_specs, check_vma=False)
```

```python
import jax
import jax.numpy as jnp
import numpy as np
from jax import lax
from jax.experimental import pallas as pl
from jax.experimental.pallas import tpu as pltpu
from jax.sharding import PartitionSpec as P

CH_IN = 4
CH_ONE = 32
CH_TWO = 64

MESH = pl.DeviceIdType.MESH
CHUNK = 32


def sum_kernel(first, second, first_out, second_out, x_ref, near, part, far, gathered, sends, recvs):
    row = lax.axis_index("gx")
    column = lax.axis_index("gy")
    sample = lax.axis_index("sa")
    me = column * 4 + sample
    barrier = pltpu.get_barrier_semaphore()

    def plane_peer(k):
        other = (me + k) % 16
        return other, (row, other // 4, other % 4)

    def row_peer(k):
        other = (row + k) % 16
        return other, (other, column, sample)

    for k in range(1, 16):
        pl.semaphore_signal(barrier, inc=1, device_id=plane_peer(k)[1], device_id_type=MESH)
        pl.semaphore_signal(barrier, inc=1, device_id=row_peer(k)[1], device_id_type=MESH)
    x_ref[...] = jnp.zeros_like(x_ref)
    for g in range(16):
        x_ref[g, 0:27] = second[:, 128 * g : 128 * g + 128]
        rows = min(2, 27 - 2 * g)
        if rows > 0:
            x_ref[g, 27 : 27 + rows] = first[2 * g : 2 * g + rows]
    pl.semaphore_wait(barrier, 30)

    def send(stage, k, source, target, device):
        copy = pltpu.make_async_remote_copy(
            src_ref=source,
            dst_ref=target,
            send_sem=sends.at[stage, k],
            recv_sem=recvs.at[stage, k],
            device_id=device,
            device_id_type=MESH,
        )
        copy.start()
        return copy

    copies = []
    for k in range(1, 16):
        other, device = plane_peer(k)
        copies.append(send(0, k, x_ref.at[other], near.at[k], device))
    total = x_ref[me]
    for k in range(1, 16):
        copies[k - 1].wait_recv()
        total = total + near[k]
    part[...] = total
    far[row] = total
    second = []
    for k in range(1, 16):
        other, device = row_peer(k)
        second.append(send(1, k, part, far.at[row], device))
    for copy in second:
        copy.wait_recv()
    total = far[0]
    for k in range(1, 16):
        total = total + far[k]
    gathered[me] = total
    third = []
    for k in range(1, 16):
        other, device = plane_peer(k)
        third.append(send(2, k, gathered.at[me], gathered.at[me], device))
    for copy in third:
        copy.wait_recv()
    for g in range(16):
        second_out[:, 128 * g : 128 * g + 128] = gathered[g, 0:27]
        rows = min(2, 27 - 2 * g)
        if rows > 0:
            first_out[2 * g : 2 * g + rows] = gathered[g, 27 : 27 + rows]
    for copy in copies + second + third:
        copy.wait_send()


def sum_over_devices(first, second):
    block = (16, CHUNK, 128)
    whole = pl.BlockSpec(memory_space=pltpu.VMEM)
    return pl.pallas_call(
        sum_kernel,
        out_shape=(
            jax.ShapeDtypeStruct(first.shape, jnp.float32),
            jax.ShapeDtypeStruct(second.shape, jnp.float32),
        ),
        in_specs=[whole, whole],
        out_specs=(whole, whole),
        scratch_shapes=[
            pltpu.VMEM(block, jnp.float32),
            pltpu.VMEM(block, jnp.float32),
            pltpu.VMEM(block[1:], jnp.float32),
            pltpu.VMEM(block, jnp.float32),
            pltpu.VMEM(block, jnp.float32),
            pltpu.SemaphoreType.DMA((3, 16)),
            pltpu.SemaphoreType.DMA((3, 16)),
        ],
        compiler_params=pltpu.CompilerParams(collective_id=0, has_side_effects=True),
        name="sum_over_devices",
    )(first, second)


def halo_kernel(volume, outer, *refs):
    outs, slots, edges, sends, recvs = refs[:8], refs[8:16], refs[16:20], refs[20], refs[21]
    row = lax.axis_index("gx")
    column = lax.axis_index("gy")
    sample = lax.axis_index("sa")
    rows = lax.axis_size("gx")
    columns = lax.axis_size("gy")

    def device(dx, dy):
        return ((row + rows + dx) % rows, (column + columns + dy) % columns, sample)

    barrier = pltpu.get_barrier_semaphore()
    around = [(dx, dy) for dx in (-1, 0, 1) for dy in (-1, 0, 1) if (dx, dy) != (0, 0)]
    for dx, dy in around:
        pl.semaphore_signal(barrier, inc=1, device_id=device(dx, dy), device_id_type=MESH)
    for whole, first, last in ((volume, *edges[:2]), (outer, *edges[2:])):
        width = first.shape[1]
        first[...] = whole[:, :width]
        last[...] = whole[:, whole.shape[1] - width :]
    pl.semaphore_wait(barrier, 8)
    copies = []

    def send(source, target, dx, dy):
        k = len(copies)
        copy = pltpu.make_async_remote_copy(
            src_ref=source,
            dst_ref=target,
            send_sem=sends.at[k],
            recv_sem=recvs.at[k],
            device_id=device(dx, dy),
            device_id_type=MESH,
        )
        copy.start()
        copies.append(copy)

    groups = (
        (volume, *edges[:2], slots[:4]),
        (outer, *edges[2:], slots[4:]),
    )
    for whole, first, last, (left, right, top, bottom) in groups:
        size = whole.shape[0]
        width = top.shape[0]
        tail = pl.ds(size - width, width)
        head = pl.ds(0, width)
        end = pl.ds(size + width, width)
        send(whole.at[tail], top, 1, 0)
        send(whole.at[head], bottom, -1, 0)
        send(last, left.at[pl.ds(width, size)], 0, 1)
        send(first, right.at[pl.ds(width, size)], 0, -1)
        send(last.at[tail], left.at[head], 1, 1)
        send(last.at[head], left.at[end], -1, 1)
        send(first.at[tail], right.at[head], 1, -1)
        send(first.at[head], right.at[end], -1, -1)
    for copy in copies:
        copy.wait_recv()
    for out, slot in zip(outs, slots):
        out[...] = slot[...]
    for copy in copies:
        copy.wait_send()


def exchange(volume, outer):
    shapes = []
    edges = []
    for x, width in ((volume, 5), (outer, 1)):
        rows, columns, lanes = x.shape
        edges += [(rows, width, lanes)] * 2
        shapes += [(rows + 2 * width, width, lanes)] * 2 + [(width, columns, lanes)] * 2
    space = pl.BlockSpec(memory_space=pltpu.VMEM)
    pieces = pl.pallas_call(
        halo_kernel,
        out_shape=tuple(jax.ShapeDtypeStruct(shape, jnp.bfloat16) for shape in shapes),
        in_specs=[space] * 2,
        out_specs=(space,) * 8,
        scratch_shapes=[pltpu.VMEM(shape, jnp.bfloat16) for shape in shapes + edges]
        + [pltpu.SemaphoreType.DMA((16,)), pltpu.SemaphoreType.DMA((16,))],
        compiler_params=pltpu.CompilerParams(collective_id=1, has_side_effects=True),
        name="exchange",
    )(volume, outer)
    result = []
    for x, (left, right, top, bottom) in ((volume, pieces[:4]), (outer, pieces[4:])):
        middle = jnp.concatenate([top, x, bottom], axis=0)
        result.append(jnp.concatenate([left, middle, right], axis=1))
    return result


PLANES_ONE = 16
PLANES_TWO = 4


def band(planes, inputs, outputs):
    rows = np.arange((planes + 2) * inputs)
    half = planes // 2 * outputs
    columns = np.arange(2 * half)
    plane = 2 * (columns % half // outputs) + columns // half
    masks = [rows[:, None] // inputs - plane[None, :] == c for c in range(3)]
    spread_rows = rows[:, None] % inputs == np.arange(inputs)[None, :]
    spread_columns = np.arange(outputs)[:, None] == columns[None, :] % outputs
    return np.stack(masks), spread_rows, spread_columns


def banded(kernel, planes, inputs, outputs):
    masks, spread_rows, spread_columns = band(planes, inputs, outputs)
    wide = jnp.dot(
        kernel.reshape(27 * inputs, outputs),
        jnp.asarray(spread_columns, jnp.bfloat16),
        preferred_element_type=jnp.bfloat16,
    ).reshape(9, 3, inputs, -1)
    spread_rows = jnp.asarray(spread_rows, jnp.bfloat16)
    full = jnp.einsum("ri,kcin->kcrn", spread_rows, wide, preferred_element_type=jnp.bfloat16)
    full = jnp.where(masks[None], full, jnp.bfloat16(0)).sum(axis=1, dtype=jnp.bfloat16)
    return full.reshape(3, 3, full.shape[1], full.shape[2])


def unbanded(grad, planes, inputs, outputs):
    masks, spread_rows, spread_columns = band(planes, inputs, outputs)
    grad = grad.reshape(9, planes + 2, inputs, -1)
    masks = masks.reshape(3, planes + 2, inputs, -1)
    parts = [jnp.where(masks[c][None], grad, 0.0).sum(axis=1) for c in range(3)]
    narrow = jnp.stack(parts, axis=1).reshape(27 * inputs, -1)
    narrow = jnp.dot(
        narrow,
        jnp.asarray(spread_columns.T, jnp.float32),
        precision=lax.Precision.HIGHEST,
        preferred_element_type=jnp.float32,
    )
    return narrow.reshape(27, inputs * outputs)


def convolve(padded, weight, padding="VALID", form="HWIO"):
    return lax.conv_general_dilated(
        padded,
        weight,
        (1, 1),
        padding,
        dimension_numbers=("NHWC", form, "NHWC"),
        preferred_element_type=jnp.float32,
    )


def weight_gradient(padded, grad):
    return lax.conv_general_dilated(
        padded,
        grad,
        (1, 1),
        "VALID",
        dimension_numbers=("CHWN", "IHWO", "HWNC"),
        preferred_element_type=jnp.float32,
    )


def average_pool(values):
    batch, rows_x, rows_y, lanes = values.shape
    values = values[..., : lanes // 2] + values[..., lanes // 2 :]
    values = values.reshape(batch, rows_x // 2, 2, rows_y // 2, 2, lanes // 2)
    return values.sum(axis=(2, 4)) * 0.125


def upsample(values):
    values = jnp.repeat(jnp.repeat(values, 2, axis=1), 2, axis=2)
    return jnp.concatenate([values, values], axis=-1)


def chunks(values, width, margin, count):
    step = width - 2 * margin
    values = jnp.pad(values, ((0, 0), (0, 0), (margin, margin)))
    return jnp.stack([values[..., j * step : j * step + width] for j in range(count)])


def merge(values):
    return jnp.concatenate(list(values), axis=-1)


def silu_slope(values):
    sigma = jax.nn.sigmoid(values)
    return sigma * (1.0 + values * (1.0 - sigma))


def body(volume, first_kernel, second_kernel, cotangent):
    weight_one = banded(first_kernel, PLANES_ONE, CH_IN, CH_ONE)
    weight_two = banded(second_kernel, PLANES_TWO, CH_ONE, CH_TWO)
    fields, outer = exchange(volume[0], cotangent[0])
    count = fields.shape[-1] // (PLANES_ONE * CH_IN)
    fields = chunks(fields, (PLANES_ONE + 2) * CH_IN, CH_IN, count)
    first_pre = convolve(fields, weight_one)
    pooled = merge(average_pool(jax.nn.silu(first_pre)).astype(jnp.bfloat16))
    pooled = chunks(pooled, (PLANES_TWO + 2) * CH_ONE, CH_ONE, 2 * count)
    second_pre = convolve(pooled, weight_two)
    inner = second_pre[:, 1:-1, 1:-1]
    result = merge(average_pool(jax.nn.silu(inner)).astype(jnp.bfloat16))
    outer = jnp.stack(jnp.split(outer, 2 * count, axis=-1))
    outer = upsample(outer)[:, 1:-1, 1:-1].astype(jnp.float32)
    second_grad = (outer * (0.125 * silu_slope(second_pre))).astype(jnp.bfloat16)
    grad_two = weight_gradient(pooled[:, 1:-1, 1:-1], second_grad[:, 1:-1, 1:-1])
    second_weights = unbanded(grad_two, PLANES_TWO, CH_ONE, CH_TWO)
    spread = convolve(second_grad, weight_two[::-1, ::-1], form="HWOI")
    middle = merge(spread[..., CH_ONE:-CH_ONE])
    below = jnp.pad(spread[1:, ..., :CH_ONE], ((0, 1), (0, 0), (0, 0), (0, 0)))
    above = jnp.pad(spread[:-1, ..., -CH_ONE:], ((1, 0), (0, 0), (0, 0), (0, 0)))
    room = ((0, 0), (0, 0), (0, 0))
    width = (PLANES_TWO - 1) * CH_ONE
    middle = middle + merge(jnp.pad(below, room + ((width, 0),)))
    middle = middle + merge(jnp.pad(above, room + ((0, width),)))
    pooled_grad = jnp.stack(jnp.split(middle, count, axis=-1))
    slope = 0.125 * silu_slope(first_pre[:, 4:-4, 4:-4])
    first_grad = (upsample(pooled_grad) * slope).astype(jnp.bfloat16)
    grad_one = weight_gradient(fields[:, 4:-4, 4:-4], first_grad)
    first_weights = unbanded(grad_one, PLANES_ONE, CH_IN, CH_ONE)
    first_weights, second_weights = sum_over_devices(first_weights, second_weights)
    return (result[None], first_weights, second_weights)


def solution(mesh):
    in_specs = (P("sa", "gx", "gy", None), P(), P(), P("sa", "gx", "gy", None))
    out_specs = (P("sa", "gx", "gy", None), P(), P())
    return jax.shard_map(body, mesh=mesh, in_specs=in_specs, out_specs=out_specs, check_vma=False)
```
